32 devices in a mesh: row: 4 (over y, core), col: 8 (over z, x).
Axes of the slice: x: 2, y: 2, z: 4, core: 2. Of those that a mesh axis runs over, the one named last changes fastest.
Arguments:
- factor: float32 [6, 2048, 6, 2048], P(None, 'row', None, 'col'), may hold values from -0.0625 to 0.0625
- diag_inv: float32 [6, 2048, 2048], P(None, None, 'row'), may hold values from -2 to 2, as said below
- structure: int32 [6, 6, 16], P(None, None, 'row'), may hold values 0 or 1
- parent: int32 [6], replicated, may hold values from 1 to 6, as said below
- post: float32 [6, 2048, 64], P(None, 'row', 'col'), may hold values from -6 to 6
Outputs:
- mean_x: float32 [6, 2048, 64], P(None, 'row', 'col')
- variance: float32 [6, 2048], P(None, 'row')
The draws below stay inside these ranges and needn't reach their ends.
Inputs may be any that keep to these rules, and one draw needn't show every extreme that they name: parent[s] > s for s < 5, and parent[5] = 6; every supernode has at most 2 ancestors, and some supernode has exactly that many. The diagonal of each diag_inv[s] lies in 0.5 to 2.
All inputs are finite; a program needn't handle non-finite values. No bound on the sum of `structure` on one device may be relied on, other than what follows from the above.
Results may differ from the reference program's by a relative error of at most 0.00014.
Values sent between devices are 32-bit elements; how exact they have to be, the bound alone decides.
A program may use at most 192 MiB of HBM per device.

```python
import math
import jax
import jax.numpy as jnp
from jax import lax

W = 2048
NSUP = 6
LEVELS = 3
RB = 128
NRHS = 64
NBLK = 16


def draw_diag_inv(key, part):
    key_lower = jax.random.fold_in(key, 11)
    key_diagonal = jax.random.fold_in(key, 12)
    lower_part = jax.random.truncated_normal(key_lower, -4.0, 4.0, (NSUP, W, W), jnp.float32) * (0.5 / math.sqrt(W))
    diagonal = jnp.exp(jax.random.uniform(key_diagonal, (NSUP, W), jnp.float32, math.log(0.5), math.log(2.0)))
    identity = jnp.eye(W, dtype=jnp.float32)
    return lower_part * (1.0 - identity) + diagonal[:, :, None] * identity


def draw_parent(key, part):
    slot_ids = jnp.arange(NSUP + 1, dtype=jnp.int32)
    parent = jnp.full((NSUP,), NSUP, jnp.int32)
    depths = jnp.zeros((NSUP + 1,), jnp.int32)
    for member in range(NSUP - 2, -1, -1):
        if member >= NSUP - LEVELS:
            chosen = jnp.int32(member + 1)
        else:
            eligible = ((slot_ids > member) & (slot_ids < NSUP) & (depths <= LEVELS - 2)).astype(jnp.int32)
            eligible_count = jnp.sum(eligible)
            drawn_slot = jax.random.randint(jax.random.fold_in(key, member), (), 0, eligible_count)
            running = jnp.cumsum(eligible)
            chosen = jnp.argmax((running == drawn_slot + 1) & (eligible == 1)).astype(jnp.int32)
        parent = parent.at[member].set(chosen)
        depths = depths.at[member].set(depths[chosen] + 1)
    return parent


def plant(array, stream_key, low, high):
    spot = [jax.random.randint(jax.random.fold_in(stream_key, axis), (), 0, length) for axis, length in enumerate(array.shape)]
    widest = array.shape.index(max(array.shape))
    neighbour = spot[:widest] + [(spot[widest] + 1) % array.shape[widest]] + spot[widest + 1:]
    return array.at[tuple(spot)].set(low).at[tuple(neighbour)].set(high)


def steps_of(stream_key, dims, shards, smallest, high):
    gain, own = 1.0, jax.random.fold_in(stream_key, 6)
    for position, shards_of in shards:
        draws = jnp.exp(jax.random.uniform(jax.random.fold_in(own, position), (shards_of,), jnp.float32, smallest / len(shards), high / len(shards)))
        gain = gain * jnp.repeat(draws, dims[position] // shards_of).reshape([-1 if axis == position else 1 for axis in range(len(dims))])
    return gain


def gaussian(rng, extent, spread, bound, shards=(), held_as=jnp.bfloat16):
    result = spread * jax.random.normal(rng, extent, jnp.float32)
    if shards:
        result = result * steps_of(rng, extent, shards, -0.22, 0.18)
    return jnp.clip(result, -bound, bound).astype(held_as)


def setup_inputs(seed: int = 0) -> dict:
    key_of = jax.random.split(jax.random.key(seed), 6)
    return {
        "factor": gaussian(key_of[0], (NSUP, W, NSUP, W), (4 * W) ** -0.5, 0.0625, ((1, 4), (3, 8)), jnp.float32),
        "diag_inv": draw_diag_inv(jax.random.fold_in(key_of[5], 71), 0),
        "structure": plant((jax.random.randint(key_of[2], (NSUP, NSUP, NBLK), 0, 4) < 3).astype(jnp.int32), jax.random.fold_in(key_of[2], 1), 0, 1),
        "parent": draw_parent(jax.random.fold_in(key_of[5], 71), 0),
        "post": gaussian(key_of[4], (NSUP, W, NRHS), 1.0, 6.0, ((1, 4), (2, 8)), jnp.float32),
    }


def ancestor_table(parent, super_count):
    extended = jnp.concatenate([parent, jnp.full((1,), super_count, jnp.int32)])
    slot_ids = jnp.arange(super_count + 1, dtype=jnp.int32)
    targets = jnp.arange(super_count, dtype=jnp.int32)
    current = parent
    table = jnp.zeros((super_count, super_count), jnp.float32)
    for hop_index in range(super_count - 1):
        table = table + (current[:, None] == targets[None, :]).astype(jnp.float32)
        onehot = (current[:, None] == slot_ids[None, :]).astype(jnp.int32)
        current = jnp.sum(onehot * extended[None, :], axis=1).astype(jnp.int32)
    return table


def reference(factor, diag_inv, structure, parent, post):
    ancestry = ancestor_table(parent, NSUP)
    row_mask = jnp.repeat(structure.astype(jnp.float32), RB, axis=2) * ancestry[:, :, None]
    lower_inv = jnp.tril(diag_inv)
    order_total = NSUP * W
    solved = [None] * NSUP
    for current_sup in range(NSUP - 1, -1, -1):
        unit_rows = jnp.eye(W, order_total, k=current_sup * W, dtype=jnp.float32)
        right = jnp.concatenate([post[current_sup], unit_rows], axis=1)
        for later in range(current_sup + 1, NSUP):
            block = factor[later, :, current_sup, :] * row_mask[current_sup, later][:, None]
            right = right - jnp.dot(block.T, solved[later], precision=lax.Precision.HIGHEST, preferred_element_type=jnp.float32)
        solved[current_sup] = jnp.dot(lower_inv[current_sup].T, right, precision=lax.Precision.HIGHEST, preferred_element_type=jnp.float32)
    solution = jnp.stack(solved)
    mean_x = solution[:, :, :NRHS]
    unit_part = solution[:, :, NRHS:]
    variance = jnp.sum(unit_part * unit_part, axis=2)
    return mean_x, variance
```

```python
import jax
import jax.numpy as jnp
from jax import lax
from jax.sharding import PartitionSpec as P

HIGH = lax.Precision.HIGH


def product(left, right):
    return jnp.dot(left, right, precision=HIGH, preferred_element_type=jnp.float32)


def body(factor, diag_inv, structure, parent, post):
    super_count = factor.shape[0]
    row_width = factor.shape[1]
    col_width = factor.shape[3]
    full_width = diag_inv.shape[1]
    row_at = lax.axis_index("row")
    col_at = lax.axis_index("col")
    last = super_count - 1
    block_rows = row_width // structure.shape[2]

    extended = jnp.concatenate([parent, jnp.full((1,), super_count, jnp.int32)])
    first_at = parent
    second_at = extended[parent]

    def pick(current_sup, target):
        clamped = jnp.minimum(target, last)
        block = lax.dynamic_index_in_dim(factor[:, :, current_sup, :], clamped, 0, keepdims=False)
        flags = lax.dynamic_index_in_dim(structure[current_sup], clamped, 0, keepdims=False)
        flags = jnp.where(target < super_count, flags.astype(jnp.float32), 0.0)
        return block * jnp.repeat(flags, block_rows)[:, None]

    blocks = [None] * super_count
    for current_sup in range(last - 1, -1, -1):
        mine = jnp.concatenate(
            [pick(current_sup, first_at[current_sup]), pick(current_sup, second_at[current_sup])], axis=0
        )
        blocks[current_sup] = lax.all_gather(mine, "col", axis=1, tiled=True)

    own_cols = row_at * row_width + jnp.arange(row_width, dtype=jnp.int32)
    rows_full = jnp.arange(full_width, dtype=jnp.int32)
    keep = rows_full[:, None] >= own_cols[None, :]
    lower = [jnp.where(keep, diag_inv[s], 0.0) for s in range(super_count)]
    unit_rows = col_at * col_width + jnp.arange(col_width, dtype=jnp.int32)
    own = lax.dynamic_slice_in_dim(diag_inv, col_at * col_width, col_width, axis=1)
    own = jnp.where((unit_rows[:, None] >= own_cols[None, :])[None], own, 0.0)
    gathered = jnp.swapaxes(lax.all_gather(post, "row", axis=1, tiled=True), 1, 2)

    def take(stacked, target):
        return lax.dynamic_index_in_dim(stacked, jnp.minimum(target, last), 0, keepdims=False)

    rhs = jnp.stack([product(gathered[s], lower[s]) for s in range(super_count)])

    def solve(current_sup, unit_part, rhs_part):
        summed = lax.psum(jnp.concatenate([unit_part, rhs_part], axis=0), "row")
        right = jnp.concatenate(
            [-summed[:col_width], gathered[current_sup] - summed[col_width:]], axis=0
        )
        fresh = product(right, lower[current_sup])
        return fresh[:col_width], fresh[col_width:]

    near = [jnp.zeros((col_width, row_width), jnp.float32)] * super_count
    means = [rhs[s] for s in range(super_count)]
    for s in range(last - 1, -1, -1):
        one, two = first_at[s], second_at[s]
        unit_part = product(take(own, one), blocks[s][:row_width])
        rhs_part = product(
            jnp.concatenate([take(rhs, one), take(rhs, two)], axis=1), blocks[s]
        )
        near[s], means[s] = solve(s, unit_part, rhs_part)
    near_all = jnp.stack(near)
    rhs = jnp.stack(means)

    far = [None] * super_count
    for s in range(last - 1, -1, -1):
        one, two = first_at[s], second_at[s]
        selected = jnp.concatenate(
            [
                jnp.concatenate([take(near_all, one), take(own, two)], axis=1),
                jnp.concatenate([take(rhs, one), take(rhs, two)], axis=1),
            ],
            axis=0,
        )
        both = product(selected, blocks[s])
        far[s], means[s] = solve(s, both[:col_width], both[col_width:])

    squares = []
    for s in range(super_count):
        total = jnp.sum(own[s] * own[s], axis=0)
        if s < last:
            total = total + jnp.sum(near[s] * near[s], axis=0) + jnp.sum(far[s] * far[s], axis=0)
        squares.append(total)
    variance = lax.psum(jnp.stack(squares), "col")
    mean_x = jnp.swapaxes(jnp.stack(means), 1, 2)
    return (mean_x, variance)


def solution(mesh):
    return jax.shard_map(
        body,
        mesh=mesh,
        in_specs=(
            P(None, "row", None, "col"),
            P(None, None, "row"),
            P(None, None, "row"),
            P(),
            P(None, "row", "col"),
        ),
        out_specs=(P(None, "row", "col"), P(None, "row")),
        check_vma=False,
    )
```
